256 devices in a mesh: region: 8 (over x, core), sector: 32 (over z, y).
Axes of the slice: x: 4, y: 4, z: 8, core: 2. Of those that a mesh axis runs over, the one named last changes fastest.
Arguments:
- psi: bfloat16 [8, 32, 256, 256], P('region', 'sector'), may hold values from -12 to 12
- left_env: bfloat16 [8, 32, 18, 256, 256], P('region', 'sector'), may hold values from -4 to 4
- right_env: bfloat16 [8, 32, 18, 256, 256], P('region', 'sector'), may hold values from -4 to 4
- diagonal: bfloat16 [8, 32, 256, 256], P('region', 'sector'), may hold values from -2 to 0
- left_coeff: float32 [18, 18], replicated, may hold values from -2 to 2
- right_coeff: float32 [18, 18], replicated, may hold values from -2 to 2
- mpo_mask: int32 [18, 18], replicated, may hold values 0 or 1
- sector_target: int32 [32, 18], P('sector'), may hold values from 0 to 31
- block_size: int32 [32], P('sector'), may hold values from 128 to 256, as said below
Outputs:
- bond: bfloat16 [8, 32, 256, 256], P('region', 'sector')
- energy: float32 [8], P('region')
The draws below stay inside these ranges and needn't reach their ends.
Inputs may be any that keep to these rules, and one draw needn't show every extreme that they name: `block_size`: one sector block has all 256 rows live, and one has exactly 128.
All inputs are finite; a program needn't handle non-finite values.
Results may differ from the reference program's by a relative error of at most 0.017.
Values may be sent and summed in bfloat16 or wider, within the bound.
No kernel may reach another device: no remote copies, remote signals or barrier semaphores. Data moves between devices by JAX's collectives and lax.ppermute only.
A program may use at most 64 MiB of HBM per device.

```python
import math
import jax
import jax.numpy as jnp
from jax import lax

BLK = 256
W = 18
ITERS = 2
NREG = 8
NSEC = 32


env_level = 0.6


def sector_scales(base, ratio):
    ramp = jnp.arange(NSEC, dtype=jnp.float32) / (NSEC - 1)
    return base * jnp.power(ratio, ramp)


def block_sizes(key):
    salted = jax.random.fold_in(key, 303)
    key_sizes, key_first, key_offset = jax.random.split(salted, 3)
    sizes = jax.random.randint(key_sizes, (NSEC,), BLK // 2, BLK + 1)
    first = jax.random.randint(key_first, (), 0, NSEC)
    second = (first + jax.random.randint(key_offset, (), 1, NSEC)) % NSEC
    places = jnp.arange(NSEC, dtype=jnp.int32)
    sizes = jnp.where(places == first, BLK, sizes)
    sizes = jnp.where(places == second, BLK // 2, sizes)
    return sizes.astype(jnp.int32)


def env_factor(key, base, ratio):
    scales = sector_scales(base, ratio)
    middle = jnp.sqrt(scales[0] * scales[-1])
    sizes = block_sizes(key).astype(jnp.float32)
    return (middle / scales) ** 2 * (BLK / sizes) * (env_level / jnp.sqrt(jnp.float32(BLK)))


def draw_env(key, salt):
    shape = (NREG, NSEC, W, BLK, BLK)
    salted = jax.random.fold_in(key, salt)
    factor = env_factor(key, 0.6, 3.0)
    values = jnp.clip(jax.random.normal(salted, shape, jnp.float32), -4.0, 4.0)
    return (values * factor[None, :, None, None, None]).astype(jnp.bfloat16)


def draw_psi(key, part):
    shape = (NREG, NSEC, BLK, BLK)
    scales = sector_scales(0.6, 3.0)
    values = jnp.clip(jax.random.normal(key, shape, jnp.float32), -5.0, 5.0)
    return (values * scales[None, :, None, None]).astype(jnp.bfloat16)


def draw_left_env(key, part):
    return draw_env(key, 101)


def draw_right_env(key, part):
    return draw_env(key, 202)


def draw_diagonal(key, part):
    shape = (NREG, NSEC, BLK, BLK)
    salted = jax.random.fold_in(key, 404)
    key_order, key_values = jax.random.split(salted)
    orders = jax.vmap(lambda one_key: jax.random.permutation(one_key, NSEC))(jax.random.split(key_order, NREG))
    lower = (orders < NSEC // 2)[:, :, None, None]
    spread = jax.random.uniform(key_values, shape, jnp.float32, 0.0, 1.0)
    low_band = -2.0 + spread
    high_band = -spread
    return jnp.where(lower, low_band, high_band).astype(jnp.bfloat16)


def draw_block_size(key, part):
    return block_sizes(key)


def place_ends(array, own_key, low, high):
    dims = array.shape
    index_at = [jax.random.randint(jax.random.fold_in(own_key, axis), (), 0, dims[axis]) for axis in range(len(dims))]
    array = array.at[tuple(index_at)].set(low)
    longest = dims.index(max(dims))
    index_at[longest] = (index_at[longest] + 1) % dims[longest]
    return array.at[tuple(index_at)].set(high)


def normal_values(own_key, extent, scale, bound, held_as=jnp.bfloat16):
    drawn = jax.random.normal(own_key, extent, jnp.float32) * scale
    return jnp.minimum(jnp.maximum(drawn, -bound), bound).astype(held_as)


def setup_inputs(seed: int = 0) -> dict:
    seeds = jax.random.split(jax.random.key(seed), 10)
    return {
        "psi": draw_psi(jax.random.fold_in(seeds[9], 71), 0),
        "left_env": draw_left_env(jax.random.fold_in(seeds[9], 71), 0),
        "right_env": draw_right_env(jax.random.fold_in(seeds[9], 71), 0),
        "diagonal": draw_diagonal(jax.random.fold_in(seeds[9], 71), 0),
        "left_coeff": normal_values(seeds[4], (W, W), (W // 2) ** -0.5, 2.0, jnp.float32),
        "right_coeff": normal_values(seeds[5], (W, W), (W // 2) ** -0.5, 2.0, jnp.float32),
        "mpo_mask": place_ends((jax.random.randint(seeds[6], (W, W), 0, 2) < 1).astype(jnp.int32), jax.random.fold_in(seeds[6], 1), 0, 1),
        "sector_target": place_ends(jax.random.randint(seeds[7], (NSEC, W), 0, NSEC), jax.random.fold_in(seeds[7], 1), 0, NSEC - 1).astype(jnp.int32),
        "block_size": draw_block_size(jax.random.fold_in(seeds[9], 71), 0),
    }


step_size = 0.5

def reference(psi, left_env, right_env, diagonal, left_coeff, right_coeff, mpo_mask, sector_target, block_size):
    highest = lax.Precision.HIGHEST
    positions = jnp.arange(BLK, dtype=jnp.int32)
    live_rows = positions[None, :] < block_size[:, None]
    keep_mask = (live_rows[:, :, None] & live_rows[:, None, :]).astype(jnp.float32)
    pattern = mpo_mask.astype(jnp.float32)
    left_mix = left_coeff * pattern
    right_mix = right_coeff * pattern
    routing = (sector_target[:, :, None] == jnp.arange(NSEC, dtype=jnp.int32)[None, None, :]).astype(jnp.float32)
    inv_root = 1.0 / math.sqrt(W)

    def prepare(items):
        psi_here, left_here, right_here = items
        masked = (psi_here.astype(jnp.float32) * keep_mask).astype(jnp.bfloat16)
        wide = masked.astype(jnp.float32)
        start_norm = jnp.sum(wide * wide)
        rescale = NSEC * BLK / start_norm
        left_half = jnp.einsum('swij,sjk->swik', left_here.astype(jnp.float32), wide).astype(jnp.bfloat16)
        left_terms = jnp.einsum('sji,swjk->swik', wide, left_half.astype(jnp.float32))
        left_out = (rescale * jnp.einsum('vw,swik->svik', left_mix, left_terms, precision=highest)).astype(jnp.bfloat16)
        right_half = jnp.einsum('swij,skj->swik', right_here.astype(jnp.float32), wide).astype(jnp.bfloat16)
        right_terms = jnp.einsum('sij,swjk->swik', wide, right_half.astype(jnp.float32))
        right_out = (rescale * jnp.einsum('vw,swik->svik', right_mix, right_terms, precision=highest)).astype(jnp.bfloat16)
        return (left_out, right_out, start_norm)
    left_out, right_out, start_norm = lax.map(prepare, (psi, left_env, right_env))

    def solve(index):
        psi_here = lax.dynamic_index_in_dim(psi, index, 0, keepdims=False)
        diag_here = lax.dynamic_index_in_dim(diagonal, index, 0, keepdims=False).astype(jnp.float32)
        before = jnp.maximum(index - 1, 0).astype(jnp.int32)
        after = jnp.minimum(index + 1, NREG - 1).astype(jnp.int32)
        left_used = jnp.where(index == 0, left_env[0], lax.dynamic_index_in_dim(left_out, before, 0, keepdims=False))
        right_used = jnp.where(index == NREG - 1, right_env[NREG - 1], lax.dynamic_index_in_dim(right_out, after, 0, keepdims=False))
        norm_here = lax.dynamic_index_in_dim(start_norm, index, 0, keepdims=False)
        masked = (psi_here.astype(jnp.float32) * keep_mask).astype(jnp.bfloat16)
        vector = (masked.astype(jnp.float32) * jnp.sqrt(NSEC * BLK * BLK / norm_here)).astype(jnp.bfloat16)
        energy = jnp.zeros((), jnp.float32)
        for step in range(ITERS):
            wide = vector.astype(jnp.float32)
            applied = jnp.einsum('swij,sjk->swik', left_used.astype(jnp.float32), wide).astype(jnp.bfloat16)
            product = jnp.einsum('swik,swkl->swil', applied.astype(jnp.float32), right_used.astype(jnp.float32))
            partial_value = jnp.einsum('swt,swil->stil', routing, product, precision=highest) * inv_root
            partial_value = lax.optimization_barrier(partial_value.astype(jnp.bfloat16)).astype(jnp.float32)
            applied_h = (lax.optimization_barrier(jnp.sum(partial_value, axis=0)) + diag_here * wide) * keep_mask
            intersection = jnp.sum(wide * wide)
            cross = jnp.sum(wide * applied_h)
            energy = cross / intersection
            update = wide - step_size * (applied_h - energy * wide)
            norm_sq = jnp.sum(update * update)
            vector = (update * jnp.sqrt(NSEC * BLK * BLK / norm_sq)).astype(jnp.bfloat16)
        return (vector, energy)
    bond, energy = lax.map(solve, jnp.arange(NREG, dtype=jnp.int32))
    return (bond, energy)
```

```python
import functools
import math

import jax
import jax.numpy as jnp
from jax import lax
from jax.experimental import pallas as pl
from jax.experimental.pallas import tpu as pltpu
from jax.sharding import Mesh
from jax.sharding import PartitionSpec as P

STEP = 0.5
ROWS_Z = 96
F32 = jnp.float32
BF16 = jnp.bfloat16
Z, Y = "z", "y"
REGION = ("x", "core")
SECTOR = ("z", "y")
VMEM_BYTES = 48 * 1024 * 1024


def along(value, axis, steps):
    count = lax.axis_size(axis)
    return lax.ppermute(value, axis, [(i, (i + steps) % count) for i in range(count)])


def exchanged(value, axis, bit):
    count = lax.axis_size(axis)
    return lax.ppermute(value, axis, [(i, i ^ bit) for i in range(count)])


def to_region(value, steps):
    count = lax.axis_size(REGION)
    leading, last = (max(0, -steps), min(count, count - steps))
    return lax.ppermute(value, REGION, [(i, i + steps) for i in range(leading, last)])


def sector_sum(value):
    for axis in (Y, Z):
        bit = 1
        while bit < lax.axis_size(axis):
            value = value + exchanged(value, axis, bit)
            bit *= 2
    return value


def add(*terms):
    total = terms[0].astype(F32)
    for term in terms[1:]:
        total = total + term.astype(F32)
    return total.astype(BF16)


def carry_kernel(mix_ref, first_ref, second_ref, env_ref, out_ref, terms_ref):
    count = env_ref.shape[0]
    width = env_ref.shape[1]
    group = 3 if count % 3 == 0 else 1

    @pl.loop(0, count // group)
    def _(step):
        for lane in range(group):
            w = step * group + lane
            half = jnp.dot(env_ref[w], first_ref[...], preferred_element_type=F32).astype(BF16)
            terms_ref[w] = jnp.dot(second_ref[...], half, preferred_element_type=F32)

    tile = 16
    block = 9 if count % 9 == 0 else count

    @pl.loop(0, width // tile)
    def _(step):
        rows = pl.ds(pl.multiple_of(step * tile, tile), tile)
        for start in range(0, count, block):
            totals = [None] * block
            for w in range(count):
                term = terms_ref[w, rows, :]
                for k in range(block):
                    part = mix_ref[start + k, w] * term
                    totals[k] = part if w == 0 else totals[k] + part
            for k in range(block):
                out_ref[start + k, rows, :] = totals[k].astype(BF16)


def carry(mix, first, second, env):
    count, width, _ = env.shape
    vmem = pl.BlockSpec(memory_space=pltpu.VMEM)
    return pl.pallas_call(
        carry_kernel,
        out_shape=jax.ShapeDtypeStruct(env.shape, BF16),
        in_specs=[pl.BlockSpec(memory_space=pltpu.SMEM), vmem, vmem, vmem],
        out_specs=vmem,
        scratch_shapes=[pltpu.VMEM((count, width, width), F32)],
        compiler_params=pltpu.CompilerParams(vmem_limit_bytes=VMEM_BYTES),
        cost_estimate=pl.CostEstimate(
            flops=4 * count * width**3, bytes_accessed=4 * count * width**2, transcendentals=0
        ),
    )(mix, first, second, env)


def apply_kernel(
    scale_ref, place_ref, target_ref,
    vector_ref, left_own, left_got, right_own, right_got,
    far_up, far_down, up2, up1, down2, down1, here, by_y,
    left_ref, right_ref, terms_ref, order_ref, first_ref, seen_ref, left_sem, right_sem,
):
    count = left_ref.shape[0]
    width = left_ref.shape[1]
    y_count, z_count = by_y.shape[0], by_y.shape[1]
    sectors = y_count * z_count
    my_z, at_start, at_end = place_ref[0], place_ref[1], place_ref[2]

    for chosen, own, got, held, sem in (
        (at_start, left_own, left_got, left_ref, left_sem),
        (at_end, right_own, right_got, right_ref, right_sem),
    ):

        @pl.when(chosen == 1)
        def _(own=own, held=held, sem=sem):
            for w in range(count):
                pltpu.make_async_copy(own.at[w], held.at[w], sem.at[w]).start()

        @pl.when(chosen != 1)
        def _(got=got, held=held, sem=sem):
            for w in range(count):
                pltpu.make_async_copy(got.at[w], held.at[w], sem.at[w]).start()

    @pl.loop(0, sectors + 1)
    def _(t):
        first_ref[t] = 0

    @pl.loop(0, count)
    def _(w):
        t = target_ref[w]
        first_ref[t + 1] = first_ref[t + 1] + 1

    @pl.loop(0, sectors)
    def _(t):
        seen_ref[t] = first_ref[t]
        first_ref[t + 1] = first_ref[t + 1] + first_ref[t]

    @pl.loop(0, count)
    def _(w):
        t = target_ref[w]
        order_ref[seen_ref[t]] = w
        seen_ref[t] = seen_ref[t] + 1

    left_scale, right_scale = scale_ref[0], scale_ref[1]
    group = 3 if count % 3 == 0 else 1

    @pl.loop(0, count // group)
    def _(step):
        for lane in range(group):
            w = step * group + lane
            pltpu.make_async_copy(left_got.at[w], left_ref.at[w], left_sem.at[w]).wait()
            pltpu.make_async_copy(right_got.at[w], right_ref.at[w], right_sem.at[w]).wait()
        for lane in range(group):
            w = step * group + lane
            applied = jnp.dot(left_ref[w], vector_ref[...], preferred_element_type=F32)
            applied = (applied * left_scale).astype(BF16)
            terms_ref[w] = jnp.dot(applied, right_ref[w], preferred_element_type=F32)

    tile = 32

    def emit(t, ref, rows_from, rows):
        low, high = first_ref[t], first_ref[t + 1]

        @pl.when(low == high)
        def _():
            ref[...] = jnp.zeros(ref.shape, BF16)

        @pl.when(low < high)
        def _():
            @pl.loop(0, rows // tile)
            def _(step):
                at = pl.multiple_of(step * tile, tile)
                source = pl.ds(rows_from + at, tile)
                total = lax.fori_loop(
                    low + 1,
                    high,
                    lambda i, total: total + terms_ref[order_ref[i], source, :],
                    terms_ref[order_ref[low], source, :],
                )
                ref[pl.ds(at, tile), :] = (total * right_scale).astype(BF16)

    z_rows = here.shape[1]
    half = y_count // 2
    for offset, parts in (
        (0, ((here, 0, 0, y_count),)),
        (1, ((up1, 0, 0, y_count),)),
        (2, ((up2, 0, 0, y_count),)),
        (3, ((far_up, half, 0, y_count),)),
        (4, ((far_up, 0, 0, half), (far_down, -half, half, y_count))),
        (5, ((far_down, half, 0, y_count),)),
        (6, ((down2, 0, 0, y_count),)),
        (7, ((down1, 0, 0, y_count),)),
    ):
        to_z = lax.rem(my_z + offset, z_count)
        for ref, shift, low_y, high_y in parts:

            @pl.loop(low_y, high_y)
            def _(to_y, ref=ref, shift=shift, to_z=to_z):
                t = to_z * y_count + to_y
                emit(t, ref.at[to_y + shift], 0, z_rows)
                emit(t, by_y.at[to_y, to_z], z_rows, width - z_rows)


def apply(scales, place, target, vector, left_own, left_got, right_own, right_got):
    count, width, _ = left_own.shape
    z_count, y_count = lax.axis_size(Z), lax.axis_size(Y)
    a, b = ROWS_Z, width - ROWS_Z
    smem = pl.BlockSpec(memory_space=pltpu.SMEM)
    vmem = pl.BlockSpec(memory_space=pltpu.VMEM)
    anywhere = pl.BlockSpec(memory_space=pl.ANY)
    near = jax.ShapeDtypeStruct((y_count, a, width), BF16)
    far = jax.ShapeDtypeStruct((y_count + y_count // 2, a, width), BF16)
    return pl.pallas_call(
        apply_kernel,
        out_shape=[far, far, near, near, near, near, near,
                   jax.ShapeDtypeStruct((y_count, z_count, b, width), BF16)],
        in_specs=[smem, smem, smem, vmem] + [anywhere] * 4,
        out_specs=[vmem] * 8,
        scratch_shapes=[
            pltpu.VMEM((count, width, width), BF16),
            pltpu.VMEM((count, width, width), BF16),
            pltpu.VMEM((count, width, width), F32),
            pltpu.SMEM((count,), jnp.int32),
            pltpu.SMEM((z_count * y_count + 1,), jnp.int32),
            pltpu.SMEM((z_count * y_count,), jnp.int32),
            pltpu.SemaphoreType.DMA((count,)),
            pltpu.SemaphoreType.DMA((count,)),
        ],
        compiler_params=pltpu.CompilerParams(vmem_limit_bytes=VMEM_BYTES),
        cost_estimate=pl.CostEstimate(
            flops=4 * count * width**3, bytes_accessed=8 * count * width**2, transcendentals=0
        ),
    )(scales, place, target, vector, left_own, left_got, right_own, right_got)


def target_sum(parts):
    far_up, far_down, up2, up1, down2, down1, here, by_y = parts
    y_count = by_y.shape[0]
    half = y_count // 2
    columns = lax.all_to_all(by_y, Y, 0, 0, tiled=True)
    from_down = along(far_up, Z, 2)
    from_up = along(far_down, Z, -2)
    send_up2 = jnp.concatenate([add(up2[:half], from_down[:half]), up2[half:]], 0)
    send_down2 = jnp.concatenate([down2[:half], add(down2[half:], from_up[:half])], 0)
    send_up1 = add(up1, from_down[half:])
    send_down1 = add(down1, from_up[half:])
    mine_z = add(
        here,
        along(send_up2, Z, 2),
        along(send_down2, Z, -2),
        along(send_up1, Z, 1),
        along(send_down1, Z, -1),
    )
    column = add(*[columns[k] for k in range(y_count)])
    rows_low = lax.all_to_all(mine_z, Y, 0, 0, tiled=True)
    rows_high = lax.all_to_all(column, Z, 0, 0, tiled=True)
    low = jnp.sum(rows_low.astype(F32), 0)
    high = jnp.sum(rows_high.astype(F32), 0)
    return jnp.concatenate([low, high], 0)


def spread(values):
    rows = [jnp.broadcast_to(v.reshape(1, 1), (1, 128)) for v in values]
    rows.append(jnp.zeros((8 - len(rows), 128), F32))
    return jnp.concatenate(rows, 0)


def local(
    psi, left_env, right_env, diagonal, left_coeff, right_coeff, mpo_mask, sector_target, block_size
):
    sectors = lax.axis_size(SECTOR)
    width = psi.shape[-1]
    count = left_env.shape[2]
    left_own, right_own = left_env[0, 0], right_env[0, 0]
    live_rows = jnp.arange(width, dtype=jnp.int32) < block_size[0]
    keep = (live_rows[:, None] & live_rows[None, :]).astype(F32)
    wide = psi[0, 0].astype(F32) * keep
    masked = wide.astype(BF16)
    turned = masked.T
    pattern = mpo_mask.astype(F32)
    region = lax.axis_index(REGION)
    at_start = region == 0
    at_end = region == lax.axis_size(REGION) - 1

    norm = jnp.broadcast_to(jnp.sum(wide * wide).reshape(1, 1), (1, 128))
    left_out = carry(left_coeff * pattern, masked, turned, left_own)
    left_got = to_region(left_out, 1)
    norm_before, norm_after = to_region(norm, 1), to_region(norm, -1)
    right_out = carry(right_coeff * pattern, turned, masked, right_own)
    right_got = to_region(right_out, -1)
    norms = jnp.concatenate([norm, norm_before, norm_after, jnp.zeros((5, 128), F32)], 0)
    norms = sector_sum(norms)

    inv_root = 1.0 / math.sqrt(count)
    cells = sectors * width * width
    left_scale = jnp.where(at_start, 1.0, sectors * width / norms[1, 0])
    right_scale = jnp.where(at_end, 1.0, sectors * width / norms[2, 0]) * inv_root
    scales = jnp.stack([left_scale, right_scale])
    place = jnp.stack(
        [lax.axis_index(Z), at_start.astype(jnp.int32), at_end.astype(jnp.int32)]
    ).astype(jnp.int32)
    diag = diagonal[0, 0].astype(F32)

    vector = (wide * jnp.sqrt(cells / norms[0, 0])).astype(BF16)
    envs = (left_own, left_got, right_own, right_got)
    current = vector.astype(F32)
    once = (target_sum(apply(scales, place, sector_target[0], vector, *envs)) + diag * current) * keep
    twice = target_sum(apply(scales, place, sector_target[0], once.astype(BF16), *envs))
    sums = sector_sum(
        spread([jnp.sum(current * current), jnp.sum(current * once), jnp.sum(once * once)])
    )
    vv, vh, hh = sums[0, 0], sums[1, 0], sums[2, 0]
    energy = vh / vv
    factor = jnp.sqrt(cells / (vv + STEP * STEP * jnp.maximum(hh - energy * vh, 0.0)))
    grow, shrink = factor * (1.0 + STEP * energy), factor * STEP

    current, applied = (
        grow * current - shrink * once,
        grow * once - shrink * ((twice + diag * once) * keep),
    )
    mine = spread(
        [jnp.sum(current * current), jnp.sum(current * applied), jnp.sum(applied * applied)]
    )
    everyone = lax.all_to_all(
        jnp.broadcast_to(mine[None], (sectors, 8, 128)), SECTOR, 0, 0, tiled=True
    )
    sums = jnp.sum(everyone, 0)
    vv, vh, hh = sums[0, 0], sums[1, 0], sums[2, 0]
    energy = vh / vv
    factor = jnp.sqrt(cells / (vv + STEP * STEP * jnp.maximum(hh - energy * vh, 0.0)))
    bond = factor * ((1.0 + STEP * energy) * current - STEP * applied)
    return bond.astype(BF16)[None, None], jnp.reshape(energy, (1,))


def solution(mesh):
    shape = (4, 2, 8, 4)
    grid = Mesh(mesh.devices.reshape(shape), ("x", "core", "z", "y"))
    blocks = functools.partial(P, REGION, SECTOR)
    in_specs = (
        blocks(None, None),
        blocks(None, None, None),
        blocks(None, None, None),
        blocks(None, None),
        P(),
        P(),
        P(),
        P(SECTOR, None),
        P(SECTOR),
    )
    out_specs = (blocks(None, None), P(REGION))
    return jax.shard_map(local, mesh=grid, in_specs=in_specs, out_specs=out_specs, check_vma=False)
```

```python
import functools
import math

import jax
import jax.numpy as jnp
from jax import lax
from jax.experimental import pallas as pl
from jax.experimental.pallas import tpu as pltpu
from jax.sharding import Mesh
from jax.sharding import PartitionSpec as P

STEP = 0.5
Z_ROWS = 128
CHUNK = 8
F32 = jnp.float32
BF16 = jnp.bfloat16
Z, Y = "z", "y"
REGION = ("x", "core")
SECTOR = ("z", "y")
SMEM_SPEC = pl.BlockSpec(memory_space=pltpu.SMEM)
VMEM_SPEC = pl.BlockSpec(memory_space=pltpu.VMEM)
HBM_SPEC = pl.BlockSpec(memory_space=pltpu.HBM)
MIB = 1024 * 1024
CARRY_PARAMS = pltpu.CompilerParams(vmem_limit_bytes=20 * MIB)
APPLY_PARAMS = pltpu.CompilerParams(vmem_limit_bytes=16 * MIB)
SMALL_PARAMS = pltpu.CompilerParams(vmem_limit_bytes=8 * MIB)


def along(value, axis, steps):
    count = lax.axis_size(axis)
    return lax.ppermute(value, axis, [(i, (i + steps) % count) for i in range(count)])


def to_region(value, steps):
    count = lax.axis_size(REGION)
    leading, last = (max(0, -steps), min(count, count - steps))
    return lax.ppermute(value, REGION, [(i, i + steps) for i in range(leading, last)])


def in_hbm(value):
    return pltpu.with_memory_space_constraint(value, pltpu.HBM)


def add(*terms):
    total = terms[0].astype(F32)
    for term in terms[1:]:
        total = total + term.astype(F32)
    return total.astype(BF16)


def after(value, *others):
    return lax.optimization_barrier((value, *others))[0]


def live(size, width):
    rows = lax.broadcasted_iota(jnp.int32, (width, width), 0) < size
    return rows & (lax.broadcasted_iota(jnp.int32, (width, width), 1) < size)


def spread_mix(coeff):
    count = coeff.shape[0]
    size = count * CHUNK

    def one_hot(shape, dim):
        at = lax.broadcasted_iota(jnp.int32, shape, dim) // CHUNK
        return (at == lax.broadcasted_iota(jnp.int32, shape, 1 - dim)).astype(F32).astype(BF16)

    down, across = one_hot((size, count), 0), one_hot((count, size), 1)
    rows = lax.broadcasted_iota(jnp.int32, (size, size), 0) % CHUNK
    same = rows == lax.broadcasted_iota(jnp.int32, (size, size), 1) % CHUNK
    high = coeff.astype(BF16)
    parts = []
    for part in (high, (coeff - high.astype(F32)).astype(BF16)):
        tall = jnp.dot(down, part, preferred_element_type=F32).astype(BF16)
        wide = jnp.dot(tall, across, preferred_element_type=F32)
        parts.append(jnp.where(same, wide, 0.0).astype(BF16))
    return jnp.concatenate(parts, 0)


def carry_kernel(
    flip, size_ref, coeff_ref, pattern_ref, psi_ref, source, target,
    env_ref, out_ref, mix_ref, first_ref, second_ref, half_ref, mixed_ref, in_sem, out_sem,
):
    count, width, _ = env_ref.shape
    pairs, chunks = count // 2, width // CHUNK
    for pair in range(pairs):
        two = pl.ds(2 * pair, 2)
        pltpu.make_async_copy(source.at[two], env_ref.at[two], in_sem.at[pair]).start()
    masked = jnp.where(live(size_ref[0], width), psi_ref[...].astype(F32), 0.0)
    turned = masked.T
    first_ref[...] = (turned if flip else masked).astype(BF16)
    second_ref[...] = (masked if flip else turned).astype(BF16)
    mix_ref[...] = spread_mix(coeff_ref[...] * pattern_ref[...].astype(F32))
    group = 3 if pairs % 3 == 0 else 1

    @pl.loop(0, pairs // group)
    def _(step):
        for lane in range(group):
            pair = step * group + lane
            two = pl.ds(2 * pair, 2)
            pltpu.make_async_copy(source.at[two], env_ref.at[two], in_sem.at[pair]).wait()
        for lane in range(group):
            pair = step * group + lane
            both = [
                jnp.dot(env_ref[2 * pair + k], first_ref[...], preferred_element_type=F32).reshape(
                    chunks, CHUNK, width
                )
                for k in range(2)
            ]
            half_ref[:, pl.ds(pair, 1)] = (
                jnp.concatenate(both, 1).astype(BF16).reshape(chunks, 1, 2 * CHUNK, width)
            )

    size = count * CHUNK
    unroll = 2

    @pl.loop(0, chunks // (2 * unroll))
    def _(step):
        for lane in range(unroll):
            two = step * unroll + lane
            both = []
            for k in range(2):
                product = jnp.dot(
                    mix_ref[...],
                    half_ref[2 * two + k].reshape(size, width),
                    preferred_element_type=F32,
                )
                both.append((product[:size] + product[size:]).reshape(count, CHUNK, width))
            rows = pl.ds(pl.multiple_of(two * 2 * CHUNK, 2 * CHUNK), 2 * CHUNK)
            mixed_ref[:, rows, :] = jnp.concatenate(both, 1).astype(BF16)

    group = 6 if count % 6 == 0 else 1

    @pl.loop(0, count // group)
    def _(step):
        for lane in range(group):
            v = step * group + lane
            out_ref[v] = jnp.dot(
                second_ref[...], mixed_ref[v], preferred_element_type=F32
            ).astype(BF16)
        done = pl.ds(step * group, group)
        pltpu.make_async_copy(out_ref.at[done], target.at[done], out_sem.at[step]).start()

    for step in range(count // group):
        done = pl.ds(step * group, group)
        pltpu.make_async_copy(out_ref.at[done], target.at[done], out_sem.at[step]).wait()


def carry(flip, size, coeff, pattern, psi, env):
    count, width, _ = env.shape
    chunks = width // CHUNK
    return pl.pallas_call(
        functools.partial(carry_kernel, flip),
        out_shape=jax.ShapeDtypeStruct(env.shape, BF16),
        in_specs=[SMEM_SPEC] + [pl.BlockSpec()] * 3 + [HBM_SPEC],
        out_specs=HBM_SPEC,
        scratch_shapes=[
            pltpu.VMEM(env.shape, BF16),
            pltpu.VMEM(env.shape, BF16),
            pltpu.VMEM((2 * count * CHUNK, count * CHUNK), BF16),
            pltpu.VMEM((width, width), BF16),
            pltpu.VMEM((width, width), BF16),
            pltpu.VMEM((chunks, count // 2, 2 * CHUNK, width), BF16),
            pltpu.VMEM((count, width, width), BF16),
            pltpu.SemaphoreType.DMA((count // 2,)),
            pltpu.SemaphoreType.DMA((count,)),
        ],
        compiler_params=CARRY_PARAMS,
        cost_estimate=pl.CostEstimate(
            flops=8 * count * width**3, bytes_accessed=4 * count * width**2, transcendentals=0
        ),
    )(size, *map(in_hbm, (coeff, pattern, psi, env)))


def slot_table(slot):
    at = jnp.arange(slot.shape[0], dtype=jnp.int32)
    before = (slot[None, :] < slot[:, None]) | (
        (slot[None, :] == slot[:, None]) & (at[None, :] < at[:, None])
    )
    rank = jnp.sum(before.astype(jnp.int32), 1)
    chosen = (rank[:, None] == at[None, :]).astype(jnp.int32)
    return jnp.stack([jnp.sum(chosen * at[:, None], 0), jnp.sum(chosen * slot[:, None], 0)])


def apply_kernel(
    row_from, ranges, place_ref, table_ref, left_norm, right_norm,
    vector_ref, left_own, left_got, right_own, right_got, *refs,
):
    out_refs = refs[: len(ranges)]
    left_ref, right_ref, total_ref, slots_ref, left_sem, right_sem, out_sem = refs[len(ranges) :]
    count, rows, width = left_ref.shape
    sectors = slots_ref.shape[0]
    at_start, at_end = place_ref[0], place_ref[1]
    part = pl.ds(row_from, rows)

    @pl.when(at_start == 1)
    def _():
        for i in range(count):
            w = table_ref[0, i]
            pltpu.make_async_copy(left_own.at[w, part], left_ref.at[i], left_sem.at[i]).start()

    @pl.when(at_start != 1)
    def _():
        for i in range(count):
            w = table_ref[0, i]
            pltpu.make_async_copy(left_got.at[w, part], left_ref.at[i], left_sem.at[i]).start()

    @pl.when(at_end == 1)
    def _():
        for i in range(count):
            w = table_ref[0, i]
            pltpu.make_async_copy(right_own.at[w], right_ref.at[i], right_sem.at[i]).start()

    @pl.when(at_end != 1)
    def _():
        for i in range(count):
            w = table_ref[0, i]
            pltpu.make_async_copy(right_got.at[w], right_ref.at[i], right_sem.at[i]).start()

    @pl.loop(0, sectors)
    def _(s):
        slots_ref[s] = jnp.zeros((rows, width), BF16)

    scale = float(sectors * width)
    one = jnp.ones((1, width), F32)
    left_scale = jnp.where(at_start == 1, one, scale / left_norm[...])
    right_scale = jnp.where(at_end == 1, one, scale / right_norm[...]) * (1.0 / math.sqrt(count))
    group = 3 if count % 3 == 0 else 1

    @pl.loop(0, count // group)
    def _(step):
        for lane in range(group):
            i = step * group + lane
            pltpu.make_async_copy(left_got.at[0, part], left_ref.at[i], left_sem.at[i]).wait()
            pltpu.make_async_copy(right_got.at[0], right_ref.at[i], right_sem.at[i]).wait()
        for lane in range(group):
            i = step * group + lane
            s = table_ref[1, i]
            fresh = (i == 0) | (s != table_ref[1, jnp.maximum(i - 1, 0)])
            applied = jnp.dot(left_ref[i], vector_ref[...], preferred_element_type=F32)
            applied = (applied * left_scale).astype(BF16)
            term = jnp.dot(applied, right_ref[i], preferred_element_type=F32)
            total = jnp.where(fresh, term, total_ref[...] + term)
            total_ref[...] = total
            slots_ref[s] = (total * right_scale).astype(BF16)

    copies = [
        pltpu.make_async_copy(slots_ref.at[pl.ds(start, size)], ref, out_sem.at[k])
        for k, ((start, size), ref) in enumerate(zip(ranges, out_refs))
    ]
    for copy in copies:
        copy.start()
    for copy in copies:
        copy.wait()


def apply(row_from, rows, ranges, place, table, norms, vector, envs):
    count, width, _ = envs[0].shape
    sectors = lax.axis_size(SECTOR)
    return pl.pallas_call(
        functools.partial(apply_kernel, row_from, ranges),
        out_shape=[jax.ShapeDtypeStruct((size, rows, width), BF16) for _, size in ranges],
        in_specs=[SMEM_SPEC, SMEM_SPEC] + [VMEM_SPEC] * 3 + [HBM_SPEC] * 4,
        out_specs=[HBM_SPEC] * len(ranges),
        scratch_shapes=[
            pltpu.VMEM((count, rows, width), BF16),
            pltpu.VMEM((count, width, width), BF16),
            pltpu.VMEM((rows, width), F32),
            pltpu.VMEM((sectors, rows, width), BF16),
            pltpu.SemaphoreType.DMA((count,)),
            pltpu.SemaphoreType.DMA((count,)),
            pltpu.SemaphoreType.DMA((len(ranges),)),
        ],
        compiler_params=APPLY_PARAMS,
        cost_estimate=pl.CostEstimate(
            flops=4 * count * rows * width**2, bytes_accessed=8 * count * width**2, transcendentals=0
        ),
    )(place, table, *norms, vector, *map(in_hbm, envs))


def add_at(value, other, start):
    room = value.shape[0] - start - other.shape[0]
    return add(value, jnp.pad(other.astype(F32), ((start, room), (0, 0), (0, 0))))


def y_ranges(y_count, z_count):
    half = z_count // 2
    return (
        (2 * z_count, half), (2 * z_count + half, z_count - half),
        (z_count, z_count), (3 * z_count, z_count), (0, z_count),
    )


def z_ranges(y_count, z_count):
    far, half = z_count // 2 * y_count, y_count // 2
    ranges = [(far, half), (far + half, y_count - half)]
    for near in range(z_count // 2 - 1, 0, -1):
        ranges += [(near * y_count, y_count), ((z_count - near) * y_count, y_count)]
    return tuple(ranges + [(0, y_count)])


def target_sums(apply_y, apply_z):
    y_up, y_down, up, down, y_here = apply_y()
    y_up_got, y_down_got = along(y_up, Y, 1), along(y_down, Y, -1)
    z_parts = apply_z()
    y_up_got, y_down_got, *z_parts = lax.optimization_barrier((y_up_got, y_down_got, *z_parts))
    z_half = z_parts[0].shape[0]
    going_up, going_down = z_parts[:2]
    for k in range(2, len(z_parts) - 1, 2):
        up_got, down_got = along(going_up, Z, 1), along(going_down, Z, -1)
        if k == 2:
            going_up, going_down = add_at(z_parts[k], up_got, 0), add_at(z_parts[k + 1], down_got, z_half)
        else:
            going_up, going_down = add(z_parts[k], up_got), add(z_parts[k + 1], down_got)
    up = add_at(up, y_up_got, 0)
    down = add_at(down, y_down_got, y_up.shape[0])
    column = add(y_here, along(up, Y, 1), along(down, Y, -1))
    column, *arrived = lax.optimization_barrier(
        (column, z_parts[-1], along(going_up, Z, 1), along(going_down, Z, -1))
    )
    high = lax.all_to_all(column, Z, 0, 0, tiled=True)
    low = [
        along(add(*[part[ahead] for part in arrived]), Y, ahead)
        for ahead in range(1, arrived[0].shape[0])
    ]
    low = sum(part.astype(F32) for part in low + [part[0] for part in arrived])
    return [low], [high]


def block_sum(size_ref, diag_ref, vector, low_count, part_refs):
    pieces = []
    for refs in (part_refs[:low_count], part_refs[low_count:]):
        terms = []
        for ref in refs:
            terms += [ref[...]] if len(ref.shape) == 2 else [ref[k] for k in range(ref.shape[0])]
        total = terms[0].astype(F32)
        for term in terms[1:]:
            total = total + term.astype(F32)
        pieces.append(total)
    total = jnp.concatenate(pieces, 0) + diag_ref[...].astype(F32) * vector
    return jnp.where(live(size_ref[0], total.shape[1]), total, 0.0)


def first_kernel(low_count, size_ref, vector_ref, diag_ref, *refs):
    *part_refs, once_ref, sent_ref = refs
    once = block_sum(size_ref, diag_ref, vector_ref[...].astype(F32), low_count, part_refs)
    once_ref[...] = once
    sent_ref[...] = once.astype(BF16)


def first_sum(size, vector, diag, low, high):
    return pl.pallas_call(
        functools.partial(first_kernel, len(low)),
        out_shape=[
            jax.ShapeDtypeStruct(vector.shape, F32),
            jax.ShapeDtypeStruct(vector.shape, BF16),
        ],
        in_specs=[SMEM_SPEC] + [pl.BlockSpec()] * (2 + len(low + high)),
        out_specs=[VMEM_SPEC] * 2,
        compiler_params=SMALL_PARAMS,
    )(size, vector, diag, *low, *high)


def total_of(value):
    return jnp.sum(jnp.sum(value, 0, keepdims=True), 1, keepdims=True)


def largest(value):
    top = jnp.max(jnp.max(jnp.abs(value), 0, keepdims=True), 1, keepdims=True)
    return jnp.maximum(top, 1e-30)


def second_kernel(low_count, size_ref, vector_ref, once_ref, diag_ref, *refs):
    *part_refs, twice_ref, moments_ref = refs
    vector = vector_ref[...].astype(F32)
    once = once_ref[...]
    twice = block_sum(size_ref, diag_ref, once, low_count, part_refs)
    twice_ref[...] = twice
    top_once, top_twice = largest(once), largest(twice)
    once, twice = once / top_once, twice / top_twice
    rows = [
        total_of(vector * vector),
        total_of(vector * once),
        total_of(once * once),
        total_of(vector * twice),
        total_of(once * twice),
        total_of(twice * twice),
        top_once,
        top_twice,
    ]
    lanes = moments_ref.shape[2]
    table = jnp.concatenate([jnp.broadcast_to(row, (1, lanes)) for row in rows], 0)
    moments_ref[...] = jnp.broadcast_to(table[None], moments_ref.shape)


def second_sum(size, vector, once, diag, low, high):
    sectors = lax.axis_size(SECTOR)
    return pl.pallas_call(
        functools.partial(second_kernel, len(low)),
        out_shape=[
            jax.ShapeDtypeStruct(vector.shape, F32),
            jax.ShapeDtypeStruct((sectors, 8, 128), F32),
        ],
        in_specs=[SMEM_SPEC] + [pl.BlockSpec()] * (3 + len(low + high)),
        out_specs=[VMEM_SPEC] * 2,
        compiler_params=SMALL_PARAMS,
    )(size, vector, once, diag, *low, *high)


def last_kernel(moments_ref, vector_ref, once_ref, twice_ref, bond_ref, energy_ref):
    sectors = moments_ref.shape[0]
    width = vector_ref.shape[0]
    cells = float(sectors * width * width)
    each = [moments_ref[:, k, :] for k in range(8)]
    top_h = jnp.max(each[6], 0, keepdims=True)
    top_g = jnp.max(each[7], 0, keepdims=True)
    h, g = each[6] / top_h, each[7] / top_g
    vv = jnp.sum(each[0], 0, keepdims=True)
    vh = jnp.sum(each[1] * h, 0, keepdims=True)
    hh = jnp.sum(each[2] * h * h, 0, keepdims=True)
    vg = jnp.sum(each[3] * g, 0, keepdims=True)
    hg = jnp.sum(each[4] * h * g, 0, keepdims=True)
    gg = jnp.sum(each[5] * g * g, 0, keepdims=True)
    energy = vh * top_h / vv
    norm = vv + STEP * STEP * jnp.maximum(top_h * (hh * top_h - energy * vh), 0.0)
    factor = jnp.sqrt(cells / norm)
    on_v = factor * (1.0 + STEP * energy)
    on_h = -STEP * factor * top_h
    to_h = on_v * top_h
    to_g = -STEP * factor * top_g
    cross = on_v * (to_h * vh + to_g * vg) + on_h * (to_h * hh + to_g * hg)
    square = to_h * (to_h * hh + 2.0 * to_g * hg) + to_g * to_g * gg
    energy = cross / cells
    norm = cells + STEP * STEP * jnp.maximum(square - energy * cross, 0.0)
    factor = jnp.sqrt(cells / norm)
    grow, shrink = factor * (1.0 + STEP * energy), factor * STEP
    energy_ref[...] = energy

    def row(value):
        return jnp.concatenate([value] * (width // value.shape[1]), 1)

    bond = row(grow * on_v) * vector_ref[...].astype(F32)
    bond = bond + row(grow * on_h - shrink * to_h) * (once_ref[...] * row(1.0 / top_h))
    bond = bond - row(shrink * to_g) * (twice_ref[...] * row(1.0 / top_g))
    bond_ref[...] = bond.astype(BF16)


def last_step(moments, vector, once, twice):
    return pl.pallas_call(
        last_kernel,
        out_shape=[
            jax.ShapeDtypeStruct(vector.shape, BF16),
            jax.ShapeDtypeStruct((1, moments.shape[2]), F32),
        ],
        in_specs=[VMEM_SPEC] * 4,
        out_specs=[VMEM_SPEC] * 2,
        compiler_params=SMALL_PARAMS,
    )(moments, vector, once, twice)


def local(
    psi, left_env, right_env, diagonal, left_coeff, right_coeff, mpo_mask, sector_target, block_size
):
    sectors = lax.axis_size(SECTOR)
    width = psi.shape[-1]
    left_own, right_own, diag = left_env[0, 0], right_env[0, 0], diagonal[0, 0]
    region = lax.axis_index(REGION)

    left_out = carry(False, block_size, left_coeff, mpo_mask, psi[0, 0], left_own)
    left_got = to_region(left_out, 1)
    right_out = carry(True, block_size, right_coeff, mpo_mask, psi[0, 0], right_own)
    right_got = to_region(right_out, -1)

    live_rows = jnp.arange(width, dtype=jnp.int32) < block_size[0]
    keep = (live_rows[:, None] & live_rows[None, :]).astype(F32)
    wide = after(psi[0, 0], right_out).astype(F32) * keep
    norm = jnp.broadcast_to(jnp.sum(wide * wide).reshape(1, 1, 1), (sectors, 8, 128))
    norm = jnp.sum(lax.all_to_all(norm, SECTOR, 0, 0, tiled=True), 0)[:1]
    norm = jnp.concatenate([norm] * (width // norm.shape[1]), 1)
    norms = to_region(norm, 1), to_region(norm, -1)
    vector = (wide * jnp.sqrt(sectors * width * width / norm)).astype(BF16)

    place = jnp.stack([region == 0, region == lax.axis_size(REGION) - 1]).astype(jnp.int32)
    z_count, y_count = lax.axis_size(Z), lax.axis_size(Y)
    to_z, to_y = sector_target[0] // y_count, sector_target[0] % y_count
    ahead_z = (to_z - lax.axis_index(Z) + z_count) % z_count
    ahead_y = (to_y - lax.axis_index(Y) + y_count) % y_count
    y_first = slot_table(ahead_y * z_count + to_z)
    z_first = slot_table(ahead_z * y_count + ahead_y)
    envs = (left_own, left_got, right_own, right_got)

    def applied(value):
        def piece(start, rows, ranges, table):
            return apply(start, rows, ranges(y_count, z_count), place, table, norms, value, envs)

        return target_sums(
            lambda: piece(Z_ROWS, width - Z_ROWS, y_ranges, y_first),
            lambda: piece(0, Z_ROWS, z_ranges, z_first),
        )

    once, sent = first_sum(block_size, vector, diag, *applied(vector))
    twice, moments = second_sum(block_size, vector, once, diag, *applied(sent))
    moments = lax.all_to_all(moments, SECTOR, 0, 0, tiled=True)
    bond, energy = last_step(moments, vector, once, twice)
    return bond[None, None], energy[0, :1]


def solution(mesh):
    shape = (4, 2, 8, 4)
    grid = Mesh(mesh.devices.reshape(shape), ("x", "core", "z", "y"))
    blocks = functools.partial(P, REGION, SECTOR)
    in_specs = (
        blocks(None, None),
        blocks(None, None, None),
        blocks(None, None, None),
        blocks(None, None),
        P(),
        P(),
        P(),
        P(SECTOR, None),
        P(SECTOR),
    )
    out_specs = (blocks(None, None), P(REGION))
    return jax.shard_map(local, mesh=grid, in_specs=in_specs, out_specs=out_specs, check_vma=False)
```

```python
import functools
import math

import jax
import jax.numpy as jnp
from jax import lax
from jax.experimental import pallas as pl
from jax.experimental.pallas import tpu as pltpu
from jax.sharding import Mesh
from jax.sharding import PartitionSpec as P

STEP = 0.5
Z_ROWS = 128
CHUNK = 8
F32 = jnp.float32
BF16 = jnp.bfloat16
Z, Y = "z", "y"
REGION = ("x", "core")
SECTOR = ("z", "y")
SMEM_SPEC = pl.BlockSpec(memory_space=pltpu.SMEM)
VMEM_SPEC = pl.BlockSpec(memory_space=pltpu.VMEM)
HBM_SPEC = pl.BlockSpec(memory_space=pltpu.HBM)
MIB = 1024 * 1024
CARRY_PARAMS = pltpu.CompilerParams(vmem_limit_bytes=20 * MIB)
APPLY_PARAMS = pltpu.CompilerParams(vmem_limit_bytes=16 * MIB)
SMALL_PARAMS = pltpu.CompilerParams(vmem_limit_bytes=8 * MIB)


def along(value, axis, steps):
    count = lax.axis_size(axis)
    return lax.ppermute(value, axis, [(i, (i + steps) % count) for i in range(count)])


def to_region(value, steps):
    count = lax.axis_size(REGION)
    leading, last = (max(0, -steps), min(count, count - steps))
    return lax.ppermute(value, REGION, [(i, i + steps) for i in range(leading, last)])


def in_hbm(value):
    return pltpu.with_memory_space_constraint(value, pltpu.HBM)


def add(*terms):
    total = terms[0].astype(F32)
    for term in terms[1:]:
        total = total + term.astype(F32)
    return total.astype(BF16)


def after(value, *others):
    return lax.optimization_barrier((value, *others))[0]


def live(size, width):
    rows = lax.broadcasted_iota(jnp.int32, (width, width), 0) < size
    return rows & (lax.broadcasted_iota(jnp.int32, (width, width), 1) < size)


def spread_mix(coeff):
    count = coeff.shape[0]
    size = count * CHUNK

    def one_hot(shape, dim):
        at = lax.broadcasted_iota(jnp.int32, shape, dim) // CHUNK
        return (at == lax.broadcasted_iota(jnp.int32, shape, 1 - dim)).astype(F32).astype(BF16)

    down, across = one_hot((size, count), 0), one_hot((count, size), 1)
    rows = lax.broadcasted_iota(jnp.int32, (size, size), 0) % CHUNK
    same = rows == lax.broadcasted_iota(jnp.int32, (size, size), 1) % CHUNK
    high = coeff.astype(BF16)
    parts = []
    for part in (high, (coeff - high.astype(F32)).astype(BF16)):
        tall = jnp.dot(down, part, preferred_element_type=F32).astype(BF16)
        wide = jnp.dot(tall, across, preferred_element_type=F32)
        parts.append(jnp.where(same, wide, 0.0).astype(BF16))
    return jnp.concatenate(parts, 0)


def carry_kernel(
    flip, size_ref, coeff_ref, pattern_ref, psi_ref, source, target,
    env_ref, out_ref, mix_ref, first_ref, second_ref, half_ref, mixed_ref, in_sem, out_sem,
):
    count, width, _ = env_ref.shape
    pairs, chunks = count // 2, width // CHUNK
    for pair in range(pairs):
        two = pl.ds(2 * pair, 2)
        pltpu.make_async_copy(source.at[two], env_ref.at[two], in_sem.at[pair]).start()
    masked = jnp.where(live(size_ref[0], width), psi_ref[...].astype(F32), 0.0)
    turned = masked.T
    first_ref[...] = (turned if flip else masked).astype(BF16)
    second_ref[...] = (masked if flip else turned).astype(BF16)
    mix_ref[...] = spread_mix(coeff_ref[...] * pattern_ref[...].astype(F32))
    group = 3 if pairs % 3 == 0 else 1

    @pl.loop(0, pairs // group)
    def _(step):
        for lane in range(group):
            pair = step * group + lane
            two = pl.ds(2 * pair, 2)
            pltpu.make_async_copy(source.at[two], env_ref.at[two], in_sem.at[pair]).wait()
        for lane in range(group):
            pair = step * group + lane
            both = [
                jnp.dot(env_ref[2 * pair + k], first_ref[...], preferred_element_type=F32).reshape(
                    chunks, CHUNK, width
                )
                for k in range(2)
            ]
            half_ref[:, pl.ds(pair, 1)] = (
                jnp.concatenate(both, 1).astype(BF16).reshape(chunks, 1, 2 * CHUNK, width)
            )

    size = count * CHUNK
    unroll = 8

    @pl.loop(0, chunks // (2 * unroll))
    def _(step):
        for lane in range(unroll):
            two = step * unroll + lane
            both = []
            for k in range(2):
                product = jnp.dot(
                    mix_ref[...],
                    half_ref[2 * two + k].reshape(size, width),
                    preferred_element_type=F32,
                )
                both.append((product[:size] + product[size:]).reshape(count, CHUNK, width))
            rows = pl.ds(pl.multiple_of(two * 2 * CHUNK, 2 * CHUNK), 2 * CHUNK)
            mixed_ref[:, rows, :] = jnp.concatenate(both, 1).astype(BF16)

    group = 6 if count % 6 == 0 else 1

    @pl.loop(0, count // group)
    def _(step):
        for lane in range(group):
            v = step * group + lane
            out_ref[v] = jnp.dot(
                second_ref[...], mixed_ref[v], preferred_element_type=F32
            ).astype(BF16)
        done = pl.ds(step * group, group)
        pltpu.make_async_copy(out_ref.at[done], target.at[done], out_sem.at[step]).start()

    for step in range(count // group):
        done = pl.ds(step * group, group)
        pltpu.make_async_copy(out_ref.at[done], target.at[done], out_sem.at[step]).wait()


def carry(flip, size, coeff, pattern, psi, env):
    count, width, _ = env.shape
    chunks = width // CHUNK
    return pl.pallas_call(
        functools.partial(carry_kernel, flip),
        out_shape=jax.ShapeDtypeStruct(env.shape, BF16),
        in_specs=[SMEM_SPEC] + [pl.BlockSpec()] * 3 + [HBM_SPEC],
        out_specs=HBM_SPEC,
        scratch_shapes=[
            pltpu.VMEM(env.shape, BF16),
            pltpu.VMEM(env.shape, BF16),
            pltpu.VMEM((2 * count * CHUNK, count * CHUNK), BF16),
            pltpu.VMEM((width, width), BF16),
            pltpu.VMEM((width, width), BF16),
            pltpu.VMEM((chunks, count // 2, 2 * CHUNK, width), BF16),
            pltpu.VMEM((count, width, width), BF16),
            pltpu.SemaphoreType.DMA((count // 2,)),
            pltpu.SemaphoreType.DMA((count,)),
        ],
        compiler_params=CARRY_PARAMS,
        cost_estimate=pl.CostEstimate(
            flops=8 * count * width**3, bytes_accessed=4 * count * width**2, transcendentals=0
        ),
    )(size, *map(in_hbm, (coeff, pattern, psi, env)))


def slot_table(slot):
    at = jnp.arange(slot.shape[0], dtype=jnp.int32)
    before = (slot[None, :] < slot[:, None]) | (
        (slot[None, :] == slot[:, None]) & (at[None, :] < at[:, None])
    )
    rank = jnp.sum(before.astype(jnp.int32), 1)
    chosen = (rank[:, None] == at[None, :]).astype(jnp.int32)
    return jnp.stack([jnp.sum(chosen * at[:, None], 0), jnp.sum(chosen * slot[:, None], 0)])


def apply_kernel(
    row_from, ranges, place_ref, table_ref, left_norm, right_norm,
    vector_ref, left_own, left_got, right_own, right_got, *refs,
):
    out_refs = refs[: len(ranges)]
    left_ref, right_ref, total_ref, slots_ref, left_sem, right_sem, out_sem = refs[len(ranges) :]
    count, rows, width = left_ref.shape
    sectors = slots_ref.shape[0]
    at_start, at_end = place_ref[0], place_ref[1]
    part = pl.ds(row_from, rows)

    @pl.when(at_start == 1)
    def _():
        for i in range(count):
            w = table_ref[0, i]
            pltpu.make_async_copy(left_own.at[w, part], left_ref.at[i], left_sem.at[i]).start()

    @pl.when(at_start != 1)
    def _():
        for i in range(count):
            w = table_ref[0, i]
            pltpu.make_async_copy(left_got.at[w, part], left_ref.at[i], left_sem.at[i]).start()

    @pl.when(at_end == 1)
    def _():
        for i in range(count):
            w = table_ref[0, i]
            pltpu.make_async_copy(right_own.at[w], right_ref.at[i], right_sem.at[i]).start()

    @pl.when(at_end != 1)
    def _():
        for i in range(count):
            w = table_ref[0, i]
            pltpu.make_async_copy(right_got.at[w], right_ref.at[i], right_sem.at[i]).start()

    @pl.loop(0, sectors)
    def _(s):
        slots_ref[s] = jnp.zeros((rows, width), BF16)

    scale = float(sectors * width)
    one = jnp.ones((1, width), F32)
    left_scale = jnp.where(at_start == 1, one, scale / left_norm[...])
    right_scale = jnp.where(at_end == 1, one, scale / right_norm[...]) * (1.0 / math.sqrt(count))
    group = 3 if count % 3 == 0 else 1

    @pl.loop(0, count // group)
    def _(step):
        for lane in range(group):
            i = step * group + lane
            pltpu.make_async_copy(left_got.at[0, part], left_ref.at[i], left_sem.at[i]).wait()
            pltpu.make_async_copy(right_got.at[0], right_ref.at[i], right_sem.at[i]).wait()
        for lane in range(group):
            i = step * group + lane
            s = table_ref[1, i]
            fresh = (i == 0) | (s != table_ref[1, jnp.maximum(i - 1, 0)])
            applied = jnp.dot(left_ref[i], vector_ref[...], preferred_element_type=F32)
            applied = (applied * left_scale).astype(BF16)
            term = jnp.dot(applied, right_ref[i], preferred_element_type=F32)
            total = jnp.where(fresh, term, total_ref[...] + term)
            total_ref[...] = total
            slots_ref[s] = (total * right_scale).astype(BF16)

    copies = [
        pltpu.make_async_copy(slots_ref.at[pl.ds(start, size)], ref, out_sem.at[k])
        for k, ((start, size), ref) in enumerate(zip(ranges, out_refs))
    ]
    for copy in copies:
        copy.start()
    for copy in copies:
        copy.wait()


def apply(row_from, rows, ranges, place, table, norms, vector, envs):
    count, width, _ = envs[0].shape
    sectors = lax.axis_size(SECTOR)
    return pl.pallas_call(
        functools.partial(apply_kernel, row_from, ranges),
        out_shape=[jax.ShapeDtypeStruct((size, rows, width), BF16) for _, size in ranges],
        in_specs=[SMEM_SPEC, SMEM_SPEC] + [VMEM_SPEC] * 3 + [HBM_SPEC] * 4,
        out_specs=[HBM_SPEC] * len(ranges),
        scratch_shapes=[
            pltpu.VMEM((count, rows, width), BF16),
            pltpu.VMEM((count, width, width), BF16),
            pltpu.VMEM((rows, width), F32),
            pltpu.VMEM((sectors, rows, width), BF16),
            pltpu.SemaphoreType.DMA((count,)),
            pltpu.SemaphoreType.DMA((count,)),
            pltpu.SemaphoreType.DMA((len(ranges),)),
        ],
        compiler_params=APPLY_PARAMS,
        cost_estimate=pl.CostEstimate(
            flops=4 * count * rows * width**2, bytes_accessed=8 * count * width**2, transcendentals=0
        ),
    )(place, table, *norms, vector, *map(in_hbm, envs))


def add_at(value, other, start):
    room = value.shape[0] - start - other.shape[0]
    return add(value, jnp.pad(other.astype(F32), ((start, room), (0, 0), (0, 0))))


def y_ranges(y_count, z_count):
    half = z_count // 2
    return (
        (2 * z_count, half), (2 * z_count + half, z_count - half),
        (z_count, z_count), (3 * z_count, z_count), (0, z_count),
    )


def z_ranges(y_count, z_count):
    far, half = z_count // 2 * y_count, y_count // 2
    ranges = [(far, half), (far + half, y_count - half)]
    for near in range(z_count // 2 - 1, 0, -1):
        ranges += [(near * y_count, y_count), ((z_count - near) * y_count, y_count)]
    return tuple(ranges + [(0, y_count)])


def target_sums(apply_y, apply_z):
    z_parts = apply_z()
    z_half = z_parts[0].shape[0]
    got = along(z_parts[0], Z, 1), along(z_parts[1], Z, -1)
    y_parts = apply_y()
    got = lax.optimization_barrier((*got, *y_parts))[:2]
    y_up, y_down, up, down, y_here = y_parts
    going_up, going_down = add_at(z_parts[2], got[0], 0), add_at(z_parts[3], got[1], z_half)
    for k in range(4, len(z_parts) - 1, 2):
        got = along(going_up, Z, 1), along(going_down, Z, -1)
        going_up, going_down = add(z_parts[k], got[0]), add(z_parts[k + 1], got[1])
    up = add_at(up, along(y_up, Y, 1), 0)
    down = add_at(down, along(y_down, Y, -1), y_up.shape[0])
    column = add(y_here, along(up, Y, 1), along(down, Y, -1))
    column, *arrived = lax.optimization_barrier(
        (column, z_parts[-1], along(going_up, Z, 1), along(going_down, Z, -1))
    )
    high = lax.all_to_all(column, Z, 0, 0, tiled=True)
    low = [
        along(add(*[part[ahead] for part in arrived]), Y, ahead)
        for ahead in range(1, arrived[0].shape[0])
    ]
    low = sum(part.astype(F32) for part in low + [part[0] for part in arrived])
    return [low], [high]


def block_sum(size_ref, diag_ref, vector, low_count, part_refs):
    pieces = []
    for refs in (part_refs[:low_count], part_refs[low_count:]):
        terms = []
        for ref in refs:
            terms += [ref[...]] if len(ref.shape) == 2 else [ref[k] for k in range(ref.shape[0])]
        total = terms[0].astype(F32)
        for term in terms[1:]:
            total = total + term.astype(F32)
        pieces.append(total)
    total = jnp.concatenate(pieces, 0) + diag_ref[...].astype(F32) * vector
    return jnp.where(live(size_ref[0], total.shape[1]), total, 0.0)


def first_kernel(low_count, size_ref, vector_ref, diag_ref, *refs):
    *part_refs, once_ref, sent_ref = refs
    once = block_sum(size_ref, diag_ref, vector_ref[...].astype(F32), low_count, part_refs)
    once_ref[...] = once
    sent_ref[...] = once.astype(BF16)


def first_sum(size, vector, diag, low, high):
    return pl.pallas_call(
        functools.partial(first_kernel, len(low)),
        out_shape=[
            jax.ShapeDtypeStruct(vector.shape, F32),
            jax.ShapeDtypeStruct(vector.shape, BF16),
        ],
        in_specs=[SMEM_SPEC] + [pl.BlockSpec()] * (2 + len(low + high)),
        out_specs=[VMEM_SPEC] * 2,
        compiler_params=SMALL_PARAMS,
    )(size, vector, diag, *low, *high)


def total_of(value):
    return jnp.sum(jnp.sum(value, 0, keepdims=True), 1, keepdims=True)


def largest(value):
    top = jnp.max(jnp.max(jnp.abs(value), 0, keepdims=True), 1, keepdims=True)
    return jnp.maximum(top, 1e-30)


def second_kernel(low_count, size_ref, vector_ref, once_ref, diag_ref, *refs):
    *part_refs, twice_ref, moments_ref = refs
    vector = vector_ref[...].astype(F32)
    once = once_ref[...]
    twice = block_sum(size_ref, diag_ref, once, low_count, part_refs)
    twice_ref[...] = twice
    top_once, top_twice = largest(once), largest(twice)
    once, twice = once / top_once, twice / top_twice
    rows = [
        total_of(vector * vector),
        total_of(vector * once),
        total_of(once * once),
        total_of(vector * twice),
        total_of(once * twice),
        total_of(twice * twice),
        top_once,
        top_twice,
    ]
    lanes = moments_ref.shape[2]
    table = jnp.concatenate([jnp.broadcast_to(row, (1, lanes)) for row in rows], 0)
    moments_ref[...] = jnp.broadcast_to(table[None], moments_ref.shape)


def second_sum(size, vector, once, diag, low, high):
    sectors = lax.axis_size(SECTOR)
    return pl.pallas_call(
        functools.partial(second_kernel, len(low)),
        out_shape=[
            jax.ShapeDtypeStruct(vector.shape, F32),
            jax.ShapeDtypeStruct((sectors, 8, 128), F32),
        ],
        in_specs=[SMEM_SPEC] + [pl.BlockSpec()] * (3 + len(low + high)),
        out_specs=[VMEM_SPEC] * 2,
        compiler_params=SMALL_PARAMS,
    )(size, vector, once, diag, *low, *high)


def last_kernel(moments_ref, vector_ref, once_ref, twice_ref, bond_ref, energy_ref):
    sectors = moments_ref.shape[0]
    width = vector_ref.shape[0]
    cells = float(sectors * width * width)
    each = [moments_ref[:, k, :] for k in range(8)]
    top_h = jnp.max(each[6], 0, keepdims=True)
    top_g = jnp.max(each[7], 0, keepdims=True)
    h, g = each[6] / top_h, each[7] / top_g
    vv = jnp.sum(each[0], 0, keepdims=True)
    vh = jnp.sum(each[1] * h, 0, keepdims=True)
    hh = jnp.sum(each[2] * h * h, 0, keepdims=True)
    vg = jnp.sum(each[3] * g, 0, keepdims=True)
    hg = jnp.sum(each[4] * h * g, 0, keepdims=True)
    gg = jnp.sum(each[5] * g * g, 0, keepdims=True)
    energy = vh * top_h / vv
    norm = vv + STEP * STEP * jnp.maximum(top_h * (hh * top_h - energy * vh), 0.0)
    factor = jnp.sqrt(cells / norm)
    on_v = factor * (1.0 + STEP * energy)
    on_h = -STEP * factor * top_h
    to_h = on_v * top_h
    to_g = -STEP * factor * top_g
    cross = on_v * (to_h * vh + to_g * vg) + on_h * (to_h * hh + to_g * hg)
    square = to_h * (to_h * hh + 2.0 * to_g * hg) + to_g * to_g * gg
    energy = cross / cells
    norm = cells + STEP * STEP * jnp.maximum(square - energy * cross, 0.0)
    factor = jnp.sqrt(cells / norm)
    grow, shrink = factor * (1.0 + STEP * energy), factor * STEP
    energy_ref[...] = energy

    def row(value):
        return jnp.concatenate([value] * (width // value.shape[1]), 1)

    bond = row(grow * on_v) * vector_ref[...].astype(F32)
    bond = bond + row(grow * on_h - shrink * to_h) * (once_ref[...] * row(1.0 / top_h))
    bond = bond - row(shrink * to_g) * (twice_ref[...] * row(1.0 / top_g))
    bond_ref[...] = bond.astype(BF16)


def last_step(moments, vector, once, twice):
    return pl.pallas_call(
        last_kernel,
        out_shape=[
            jax.ShapeDtypeStruct(vector.shape, BF16),
            jax.ShapeDtypeStruct((1, moments.shape[2]), F32),
        ],
        in_specs=[VMEM_SPEC] * 4,
        out_specs=[VMEM_SPEC] * 2,
        compiler_params=SMALL_PARAMS,
    )(moments, vector, once, twice)


def local(
    psi, left_env, right_env, diagonal, left_coeff, right_coeff, mpo_mask, sector_target, block_size
):
    sectors = lax.axis_size(SECTOR)
    width = psi.shape[-1]
    left_own, right_own, diag = left_env[0, 0], right_env[0, 0], diagonal[0, 0]
    region = lax.axis_index(REGION)

    left_out = carry(False, block_size, left_coeff, mpo_mask, psi[0, 0], left_own)
    left_got = to_region(left_out, 1)
    right_out = carry(True, block_size, right_coeff, mpo_mask, psi[0, 0], right_own)
    right_got = to_region(right_out, -1)

    live_rows = jnp.arange(width, dtype=jnp.int32) < block_size[0]
    keep = (live_rows[:, None] & live_rows[None, :]).astype(F32)
    wide = after(psi[0, 0], right_out).astype(F32) * keep
    norm = jnp.broadcast_to(jnp.sum(wide * wide).reshape(1, 1, 1), (sectors, 8, 128))
    norm = jnp.sum(lax.all_to_all(norm, SECTOR, 0, 0, tiled=True), 0)[:1]
    norm = jnp.concatenate([norm] * (width // norm.shape[1]), 1)
    norms = to_region(norm, 1), to_region(norm, -1)
    vector = (wide * jnp.sqrt(sectors * width * width / norm)).astype(BF16)

    place = jnp.stack([region == 0, region == lax.axis_size(REGION) - 1]).astype(jnp.int32)
    z_count, y_count = lax.axis_size(Z), lax.axis_size(Y)
    to_z, to_y = sector_target[0] // y_count, sector_target[0] % y_count
    ahead_z = (to_z - lax.axis_index(Z) + z_count) % z_count
    ahead_y = (to_y - lax.axis_index(Y) + y_count) % y_count
    y_first = slot_table(ahead_y * z_count + to_z)
    z_first = slot_table(ahead_z * y_count + ahead_y)
    envs = (left_own, left_got, right_own, right_got)

    def applied(value):
        def piece(start, rows, ranges, table):
            return apply(start, rows, ranges(y_count, z_count), place, table, norms, value, envs)

        return target_sums(
            lambda: piece(Z_ROWS, width - Z_ROWS, y_ranges, y_first),
            lambda: piece(0, Z_ROWS, z_ranges, z_first),
        )

    once, sent = first_sum(block_size, vector, diag, *applied(vector))
    twice, moments = second_sum(block_size, vector, once, diag, *applied(sent))
    moments = lax.all_to_all(moments, SECTOR, 0, 0, tiled=True)
    bond, energy = last_step(moments, vector, once, twice)
    return bond[None, None], energy[0, :1]


def solution(mesh):
    shape = (4, 2, 8, 4)
    grid = Mesh(mesh.devices.reshape(shape), ("x", "core", "z", "y"))
    blocks = functools.partial(P, REGION, SECTOR)
    in_specs = (
        blocks(None, None),
        blocks(None, None, None),
        blocks(None, None, None),
        blocks(None, None),
        P(),
        P(),
        P(),
        P(SECTOR, None),
        P(SECTOR),
    )
    out_specs = (blocks(None, None), P(REGION))
    return jax.shard_map(local, mesh=grid, in_specs=in_specs, out_specs=out_specs, check_vma=False)
```

```python
import functools
import math

import jax
import jax.numpy as jnp
from jax import lax
from jax.experimental import pallas as pl
from jax.experimental.pallas import tpu as pltpu
from jax.sharding import Mesh
from jax.sharding import PartitionSpec as P

STEP = 0.5
Z_ROWS = 128
CHUNK = 8
F32 = jnp.float32
BF16 = jnp.bfloat16
Z, Y = "z", "y"
REGION = ("x", "core")
SECTOR = ("z", "y")
SMEM_SPEC = pl.BlockSpec(memory_space=pltpu.SMEM)
VMEM_SPEC = pl.BlockSpec(memory_space=pltpu.VMEM)
HBM_SPEC = pl.BlockSpec(memory_space=pltpu.HBM)
MIB = 1024 * 1024
CARRY_PARAMS = pltpu.CompilerParams(vmem_limit_bytes=20 * MIB)
APPLY_PARAMS = pltpu.CompilerParams(vmem_limit_bytes=16 * MIB)
SMALL_PARAMS = pltpu.CompilerParams(vmem_limit_bytes=8 * MIB)


def along(value, axis, steps):
    count = lax.axis_size(axis)
    return lax.ppermute(value, axis, [(i, (i + steps) % count) for i in range(count)])


def to_region(value, steps):
    count = lax.axis_size(REGION)
    leading, last = (max(0, -steps), min(count, count - steps))
    return lax.ppermute(value, REGION, [(i, i + steps) for i in range(leading, last)])


def in_hbm(value):
    return pltpu.with_memory_space_constraint(value, pltpu.HBM)


def add(*terms):
    total = terms[0].astype(F32)
    for term in terms[1:]:
        total = total + term.astype(F32)
    return total.astype(BF16)


def after(value, *others):
    return lax.optimization_barrier((value, *others))[0]


def live(size, width):
    rows = lax.broadcasted_iota(jnp.int32, (width, width), 0) < size
    return rows & (lax.broadcasted_iota(jnp.int32, (width, width), 1) < size)


def spread_mix(coeff):
    count = coeff.shape[0]
    size = count * CHUNK

    def one_hot(shape, dim):
        at = lax.broadcasted_iota(jnp.int32, shape, dim) // CHUNK
        return (at == lax.broadcasted_iota(jnp.int32, shape, 1 - dim)).astype(F32).astype(BF16)

    down, across = one_hot((size, count), 0), one_hot((count, size), 1)
    rows = lax.broadcasted_iota(jnp.int32, (size, size), 0) % CHUNK
    same = rows == lax.broadcasted_iota(jnp.int32, (size, size), 1) % CHUNK
    high = coeff.astype(BF16)
    parts = []
    for part in (high, (coeff - high.astype(F32)).astype(BF16)):
        tall = jnp.dot(down, part, preferred_element_type=F32).astype(BF16)
        wide = jnp.dot(tall, across, preferred_element_type=F32)
        parts.append(jnp.where(same, wide, 0.0).astype(BF16))
    return jnp.concatenate(parts, 0)


def carry_kernel(
    flip, size_ref, coeff_from, pattern_from, psi_from, source, target,
    env_ref, out_ref, mix_ref, first_ref, second_ref, half_ref, mixed_ref,
    coeff_ref, pattern_ref, psi_ref, in_sem, out_sem, small_sem,
):
    count, width, _ = env_ref.shape
    pairs, chunks = count // 2, width // CHUNK
    small = [
        pltpu.make_async_copy(here, there, small_sem.at[k])
        for k, (here, there) in enumerate(
            ((psi_from, psi_ref), (coeff_from, coeff_ref), (pattern_from, pattern_ref))
        )
    ]
    for copy in small:
        copy.start()
    for pair in range(pairs):
        two = pl.ds(2 * pair, 2)
        pltpu.make_async_copy(source.at[two], env_ref.at[two], in_sem.at[pair]).start()
    for copy in small:
        copy.wait()
    masked = jnp.where(live(size_ref[0], width), psi_ref[...].astype(F32), 0.0)
    turned = masked.T
    first_ref[...] = (turned if flip else masked).astype(BF16)
    second_ref[...] = (masked if flip else turned).astype(BF16)
    mix_ref[...] = spread_mix(coeff_ref[...] * pattern_ref[...].astype(F32))
    group = 3 if pairs % 3 == 0 else 1

    @pl.loop(0, pairs // group)
    def _(step):
        for lane in range(group):
            pair = step * group + lane
            two = pl.ds(2 * pair, 2)
            pltpu.make_async_copy(source.at[two], env_ref.at[two], in_sem.at[pair]).wait()
        for lane in range(group):
            pair = step * group + lane
            both = [
                jnp.dot(env_ref[2 * pair + k], first_ref[...], preferred_element_type=F32).reshape(
                    chunks, CHUNK, width
                )
                for k in range(2)
            ]
            half_ref[:, pl.ds(pair, 1)] = (
                jnp.concatenate(both, 1).astype(BF16).reshape(chunks, 1, 2 * CHUNK, width)
            )

    size = count * CHUNK
    unroll = 8

    @pl.loop(0, chunks // (2 * unroll))
    def _(step):
        for lane in range(unroll):
            two = step * unroll + lane
            both = []
            for k in range(2):
                product = jnp.dot(
                    mix_ref[...],
                    half_ref[2 * two + k].reshape(size, width),
                    preferred_element_type=F32,
                )
                both.append((product[:size] + product[size:]).reshape(count, CHUNK, width))
            rows = pl.ds(pl.multiple_of(two * 2 * CHUNK, 2 * CHUNK), 2 * CHUNK)
            mixed_ref[:, rows, :] = jnp.concatenate(both, 1).astype(BF16)

    group = 6 if count % 6 == 0 else 1

    @pl.loop(0, count // group)
    def _(step):
        for lane in range(group):
            v = step * group + lane
            out_ref[v] = jnp.dot(
                second_ref[...], mixed_ref[v], preferred_element_type=F32
            ).astype(BF16)
        done = pl.ds(step * group, group)
        pltpu.make_async_copy(out_ref.at[done], target.at[done], out_sem.at[step]).start()

    for step in range(count // group):
        done = pl.ds(step * group, group)
        pltpu.make_async_copy(out_ref.at[done], target.at[done], out_sem.at[step]).wait()


def carry(flip, size, coeff, pattern, psi, env):
    count, width, _ = env.shape
    chunks = width // CHUNK
    return pl.pallas_call(
        functools.partial(carry_kernel, flip),
        out_shape=jax.ShapeDtypeStruct(env.shape, BF16),
        in_specs=[SMEM_SPEC] + [HBM_SPEC] * 4,
        out_specs=HBM_SPEC,
        scratch_shapes=[
            pltpu.VMEM(env.shape, BF16),
            pltpu.VMEM(env.shape, BF16),
            pltpu.VMEM((2 * count * CHUNK, count * CHUNK), BF16),
            pltpu.VMEM((width, width), BF16),
            pltpu.VMEM((width, width), BF16),
            pltpu.VMEM((chunks, count // 2, 2 * CHUNK, width), BF16),
            pltpu.VMEM((count, width, width), BF16),
            pltpu.VMEM(coeff.shape, F32),
            pltpu.VMEM(pattern.shape, jnp.int32),
            pltpu.VMEM(psi.shape, BF16),
            pltpu.SemaphoreType.DMA((count // 2,)),
            pltpu.SemaphoreType.DMA((count,)),
            pltpu.SemaphoreType.DMA((3,)),
        ],
        compiler_params=CARRY_PARAMS,
        cost_estimate=pl.CostEstimate(
            flops=8 * count * width**3, bytes_accessed=4 * count * width**2, transcendentals=0
        ),
    )(size, *map(in_hbm, (coeff, pattern, psi, env)))


def slot_table(slot):
    at = jnp.arange(slot.shape[0], dtype=jnp.int32)
    before = (slot[None, :] < slot[:, None]) | (
        (slot[None, :] == slot[:, None]) & (at[None, :] < at[:, None])
    )
    rank = jnp.sum(before.astype(jnp.int32), 1)
    chosen = (rank[:, None] == at[None, :]).astype(jnp.int32)
    return jnp.stack([jnp.sum(chosen * at[:, None], 0), jnp.sum(chosen * slot[:, None], 0)])


def apply_kernel(
    row_from, ranges, place_ref, table_ref, left_norm, right_norm,
    vector_ref, left_own, left_got, right_own, right_got, *refs,
):
    out_refs = refs[: len(ranges)]
    left_ref, right_ref, total_ref, slots_ref, left_sem, right_sem, out_sem = refs[len(ranges) :]
    count, rows, width = left_ref.shape
    sectors = slots_ref.shape[0]
    at_start, at_end = place_ref[0], place_ref[1]
    part = pl.ds(row_from, rows)

    @pl.when(at_start == 1)
    def _():
        for i in range(count):
            w = table_ref[0, i]
            pltpu.make_async_copy(left_own.at[w, part], left_ref.at[i], left_sem.at[i]).start()

    @pl.when(at_start != 1)
    def _():
        for i in range(count):
            w = table_ref[0, i]
            pltpu.make_async_copy(left_got.at[w, part], left_ref.at[i], left_sem.at[i]).start()

    @pl.when(at_end == 1)
    def _():
        for i in range(count):
            w = table_ref[0, i]
            pltpu.make_async_copy(right_own.at[w], right_ref.at[i], right_sem.at[i]).start()

    @pl.when(at_end != 1)
    def _():
        for i in range(count):
            w = table_ref[0, i]
            pltpu.make_async_copy(right_got.at[w], right_ref.at[i], right_sem.at[i]).start()

    @pl.loop(0, sectors)
    def _(s):
        slots_ref[s] = jnp.zeros((rows, width), BF16)

    scale = float(sectors * width)
    one = jnp.ones((1, width), F32)
    left_scale = jnp.where(at_start == 1, one, scale / left_norm[...])
    right_scale = jnp.where(at_end == 1, one, scale / right_norm[...]) * (1.0 / math.sqrt(count))
    group = 3 if count % 3 == 0 else 1

    @pl.loop(0, count // group)
    def _(step):
        for lane in range(group):
            i = step * group + lane
            pltpu.make_async_copy(left_got.at[0, part], left_ref.at[i], left_sem.at[i]).wait()
            pltpu.make_async_copy(right_got.at[0], right_ref.at[i], right_sem.at[i]).wait()
        for lane in range(group):
            i = step * group + lane
            s = table_ref[1, i]
            fresh = (i == 0) | (s != table_ref[1, jnp.maximum(i - 1, 0)])
            applied = jnp.dot(left_ref[i], vector_ref[...], preferred_element_type=F32)
            applied = (applied * left_scale).astype(BF16)
            term = jnp.dot(applied, right_ref[i], preferred_element_type=F32)
            total = jnp.where(fresh, term, total_ref[...] + term)
            total_ref[...] = total
            slots_ref[s] = (total * right_scale).astype(BF16)

    copies = [
        pltpu.make_async_copy(slots_ref.at[pl.ds(start, size)], ref, out_sem.at[k])
        for k, ((start, size), ref) in enumerate(zip(ranges, out_refs))
    ]
    for copy in copies:
        copy.start()
    for copy in copies:
        copy.wait()


def apply(row_from, rows, ranges, place, table, norms, vector, envs):
    count, width, _ = envs[0].shape
    sectors = lax.axis_size(SECTOR)
    return pl.pallas_call(
        functools.partial(apply_kernel, row_from, ranges),
        out_shape=[jax.ShapeDtypeStruct((size, rows, width), BF16) for _, size in ranges],
        in_specs=[SMEM_SPEC, SMEM_SPEC] + [VMEM_SPEC] * 3 + [HBM_SPEC] * 4,
        out_specs=[HBM_SPEC] * len(ranges),
        scratch_shapes=[
            pltpu.VMEM((count, rows, width), BF16),
            pltpu.VMEM((count, width, width), BF16),
            pltpu.VMEM((rows, width), F32),
            pltpu.VMEM((sectors, rows, width), BF16),
            pltpu.SemaphoreType.DMA((count,)),
            pltpu.SemaphoreType.DMA((count,)),
            pltpu.SemaphoreType.DMA((len(ranges),)),
        ],
        compiler_params=APPLY_PARAMS,
        cost_estimate=pl.CostEstimate(
            flops=4 * count * rows * width**2, bytes_accessed=8 * count * width**2, transcendentals=0
        ),
    )(place, table, *norms, vector, *map(in_hbm, envs))


def add_at(value, other, start):
    room = value.shape[0] - start - other.shape[0]
    return add(value, jnp.pad(other.astype(F32), ((start, room), (0, 0), (0, 0))))


def y_ranges(y_count, z_count):
    half = z_count // 2
    return (
        (2 * z_count, half), (2 * z_count + half, z_count - half),
        (z_count, z_count), (3 * z_count, z_count), (0, z_count),
    )


def z_ranges(y_count, z_count):
    far, half = z_count // 2 * y_count, y_count // 2
    ranges = [(far, half), (far + half, y_count - half)]
    for near in range(z_count // 2 - 1, 0, -1):
        ranges += [(near * y_count, y_count), ((z_count - near) * y_count, y_count)]
    return tuple(ranges + [(0, y_count)])


def target_sums(apply_y, apply_z):
    z_parts = apply_z()
    z_half = z_parts[0].shape[0]
    got = along(z_parts[0], Z, 1), along(z_parts[1], Z, -1)
    y_parts = apply_y()
    got = lax.optimization_barrier((*got, *y_parts))[:2]
    y_up, y_down, up, down, y_here = y_parts
    going_up, going_down = add_at(z_parts[2], got[0], 0), add_at(z_parts[3], got[1], z_half)
    for k in range(4, len(z_parts) - 1, 2):
        got = along(going_up, Z, 1), along(going_down, Z, -1)
        going_up, going_down = add(z_parts[k], got[0]), add(z_parts[k + 1], got[1])
    up = add_at(up, along(y_up, Y, 1), 0)
    down = add_at(down, along(y_down, Y, -1), y_up.shape[0])
    column = add(y_here, along(up, Y, 1), along(down, Y, -1))
    column, *arrived = lax.optimization_barrier(
        (column, z_parts[-1], along(going_up, Z, 1), along(going_down, Z, -1))
    )
    high = lax.all_to_all(column, Z, 0, 0, tiled=True)
    low = [
        along(add(*[part[ahead] for part in arrived]), Y, ahead)
        for ahead in range(1, arrived[0].shape[0])
    ]
    low = sum(part.astype(F32) for part in low + [part[0] for part in arrived])
    return [low], [high]


def block_sum(size_ref, diag_ref, vector, low_count, part_refs):
    pieces = []
    for refs in (part_refs[:low_count], part_refs[low_count:]):
        terms = []
        for ref in refs:
            terms += [ref[...]] if len(ref.shape) == 2 else [ref[k] for k in range(ref.shape[0])]
        total = terms[0].astype(F32)
        for term in terms[1:]:
            total = total + term.astype(F32)
        pieces.append(total)
    total = jnp.concatenate(pieces, 0) + diag_ref[...].astype(F32) * vector
    return jnp.where(live(size_ref[0], total.shape[1]), total, 0.0)


def first_kernel(low_count, size_ref, vector_ref, diag_ref, *refs):
    *part_refs, once_ref, sent_ref = refs
    once = block_sum(size_ref, diag_ref, vector_ref[...].astype(F32), low_count, part_refs)
    once_ref[...] = once
    sent_ref[...] = once.astype(BF16)


def first_sum(size, vector, diag, low, high):
    return pl.pallas_call(
        functools.partial(first_kernel, len(low)),
        out_shape=[
            jax.ShapeDtypeStruct(vector.shape, F32),
            jax.ShapeDtypeStruct(vector.shape, BF16),
        ],
        in_specs=[SMEM_SPEC] + [pl.BlockSpec()] * (2 + len(low + high)),
        out_specs=[VMEM_SPEC] * 2,
        compiler_params=SMALL_PARAMS,
    )(size, vector, diag, *low, *high)


def total_of(value):
    return jnp.sum(jnp.sum(value, 0, keepdims=True), 1, keepdims=True)


def largest(value):
    top = jnp.max(jnp.max(jnp.abs(value), 0, keepdims=True), 1, keepdims=True)
    return jnp.maximum(top, 1e-30)


def second_kernel(low_count, size_ref, vector_ref, once_ref, diag_ref, *refs):
    *part_refs, twice_ref, moments_ref = refs
    vector = vector_ref[...].astype(F32)
    once = once_ref[...]
    twice = block_sum(size_ref, diag_ref, once, low_count, part_refs)
    twice_ref[...] = twice
    top_once, top_twice = largest(once), largest(twice)
    once, twice = once / top_once, twice / top_twice
    rows = [
        total_of(vector * vector),
        total_of(vector * once),
        total_of(once * once),
        total_of(vector * twice),
        total_of(once * twice),
        total_of(twice * twice),
        top_once,
        top_twice,
    ]
    lanes = moments_ref.shape[2]
    table = jnp.concatenate([jnp.broadcast_to(row, (1, lanes)) for row in rows], 0)
    moments_ref[...] = jnp.broadcast_to(table[None], moments_ref.shape)


def second_sum(size, vector, once, diag, low, high):
    sectors = lax.axis_size(SECTOR)
    return pl.pallas_call(
        functools.partial(second_kernel, len(low)),
        out_shape=[
            jax.ShapeDtypeStruct(vector.shape, F32),
            jax.ShapeDtypeStruct((sectors, 8, 128), F32),
        ],
        in_specs=[SMEM_SPEC] + [pl.BlockSpec()] * (3 + len(low + high)),
        out_specs=[VMEM_SPEC] * 2,
        compiler_params=SMALL_PARAMS,
    )(size, vector, once, diag, *low, *high)


def last_kernel(moments_ref, vector_ref, once_ref, twice_ref, bond_ref, energy_ref):
    sectors = moments_ref.shape[0]
    width = vector_ref.shape[0]
    cells = float(sectors * width * width)
    each = [moments_ref[:, k, :] for k in range(8)]
    top_h = jnp.max(each[6], 0, keepdims=True)
    top_g = jnp.max(each[7], 0, keepdims=True)
    h, g = each[6] / top_h, each[7] / top_g
    vv = jnp.sum(each[0], 0, keepdims=True)
    vh = jnp.sum(each[1] * h, 0, keepdims=True)
    hh = jnp.sum(each[2] * h * h, 0, keepdims=True)
    vg = jnp.sum(each[3] * g, 0, keepdims=True)
    hg = jnp.sum(each[4] * h * g, 0, keepdims=True)
    gg = jnp.sum(each[5] * g * g, 0, keepdims=True)
    energy = vh * top_h / vv
    norm = vv + STEP * STEP * jnp.maximum(top_h * (hh * top_h - energy * vh), 0.0)
    factor = jnp.sqrt(cells / norm)
    on_v = factor * (1.0 + STEP * energy)
    on_h = -STEP * factor * top_h
    to_h = on_v * top_h
    to_g = -STEP * factor * top_g
    cross = on_v * (to_h * vh + to_g * vg) + on_h * (to_h * hh + to_g * hg)
    square = to_h * (to_h * hh + 2.0 * to_g * hg) + to_g * to_g * gg
    energy = cross / cells
    norm = cells + STEP * STEP * jnp.maximum(square - energy * cross, 0.0)
    factor = jnp.sqrt(cells / norm)
    grow, shrink = factor * (1.0 + STEP * energy), factor * STEP
    energy_ref[...] = energy

    def row(value):
        return jnp.concatenate([value] * (width // value.shape[1]), 1)

    bond = row(grow * on_v) * vector_ref[...].astype(F32)
    bond = bond + row(grow * on_h - shrink * to_h) * (once_ref[...] * row(1.0 / top_h))
    bond = bond - row(shrink * to_g) * (twice_ref[...] * row(1.0 / top_g))
    bond_ref[...] = bond.astype(BF16)


def last_step(moments, vector, once, twice):
    return pl.pallas_call(
        last_kernel,
        out_shape=[
            jax.ShapeDtypeStruct(vector.shape, BF16),
            jax.ShapeDtypeStruct((1, moments.shape[2]), F32),
        ],
        in_specs=[VMEM_SPEC] * 4,
        out_specs=[VMEM_SPEC] * 2,
        compiler_params=SMALL_PARAMS,
    )(moments, vector, once, twice)


def local(
    psi, left_env, right_env, diagonal, left_coeff, right_coeff, mpo_mask, sector_target, block_size
):
    sectors = lax.axis_size(SECTOR)
    width = psi.shape[-1]
    left_own, right_own, diag = left_env[0, 0], right_env[0, 0], diagonal[0, 0]
    region = lax.axis_index(REGION)

    left_out = carry(False, block_size, left_coeff, mpo_mask, psi[0, 0], left_own)
    left_got = to_region(left_out, 1)
    right_out = carry(True, block_size, right_coeff, mpo_mask, psi[0, 0], right_own)
    right_got = to_region(right_out, -1)

    live_rows = jnp.arange(width, dtype=jnp.int32) < block_size[0]
    keep = (live_rows[:, None] & live_rows[None, :]).astype(F32)
    wide = after(psi[0, 0], right_out).astype(F32) * keep
    norm = jnp.broadcast_to(jnp.sum(wide * wide).reshape(1, 1, 1), (sectors, 8, 128))
    norm = jnp.sum(lax.all_to_all(norm, SECTOR, 0, 0, tiled=True), 0)[:1]
    norm = jnp.concatenate([norm] * (width // norm.shape[1]), 1)
    norms = to_region(norm, 1), to_region(norm, -1)
    vector = (wide * jnp.sqrt(sectors * width * width / norm)).astype(BF16)

    place = jnp.stack([region == 0, region == lax.axis_size(REGION) - 1]).astype(jnp.int32)
    z_count, y_count = lax.axis_size(Z), lax.axis_size(Y)
    to_z, to_y = sector_target[0] // y_count, sector_target[0] % y_count
    ahead_z = (to_z - lax.axis_index(Z) + z_count) % z_count
    ahead_y = (to_y - lax.axis_index(Y) + y_count) % y_count
    y_first = slot_table(ahead_y * z_count + to_z)
    z_first = slot_table(ahead_z * y_count + ahead_y)
    envs = (left_own, left_got, right_own, right_got)

    def applied(value):
        def piece(start, rows, ranges, table):
            return apply(start, rows, ranges(y_count, z_count), place, table, norms, value, envs)

        return target_sums(
            lambda: piece(Z_ROWS, width - Z_ROWS, y_ranges, y_first),
            lambda: piece(0, Z_ROWS, z_ranges, z_first),
        )

    once, sent = first_sum(block_size, vector, diag, *applied(vector))
    twice, moments = second_sum(block_size, vector, once, diag, *applied(sent))
    moments = lax.all_to_all(moments, SECTOR, 0, 0, tiled=True)
    bond, energy = last_step(moments, vector, once, twice)
    return bond[None, None], energy[0, :1]


def solution(mesh):
    shape = (4, 2, 8, 4)
    grid = Mesh(mesh.devices.reshape(shape), ("x", "core", "z", "y"))
    blocks = functools.partial(P, REGION, SECTOR)
    in_specs = (
        blocks(None, None),
        blocks(None, None, None),
        blocks(None, None, None),
        blocks(None, None),
        P(),
        P(),
        P(),
        P(SECTOR, None),
        P(SECTOR),
    )
    out_specs = (blocks(None, None), P(REGION))
    return jax.shard_map(local, mesh=grid, in_specs=in_specs, out_specs=out_specs, check_vma=False)
```
